32 devices in a mesh: grp: 8 (over z, x), sub: 4 (over y, core).
Axes of the slice: x: 2, y: 2, z: 4, core: 2. Of those that a mesh axis runs over, the one named last changes fastest.
Arguments:
- ham_columns: bfloat16 [96, 5, 128, 128], P(('grp', 'sub')), may hold values from -2.2 to 2.2, as said below
- bond_mask: int32 [96, 4], P(('grp', 'sub')), may hold values 0 or 1
- owned_counts: int32 [8, 4], replicated, may hold values from 1 to 3, as said below
- fermi_level: float32 [1], replicated, may hold values from -0.5 to 0.5
Outputs:
- density: bfloat16 [96, 9, 128, 128], P(('grp', 'sub'))
The draws below stay inside these ranges and needn't reach their ends.
Inputs may be any that keep to these rules, and one draw needn't show every extreme that they name: `ham_columns`: block 0 of every stored block column is symmetric. `bond_mask`: bond lists of slots that hold no cluster are never read. `owned_counts`: along sub, the devices 2k and 2k + 1 of a group own 2 * 2 block columns together, so group g owns clusters g * 8 to (g + 1) * 8 - 1, handed to its devices in order along sub in consecutive runs; no device owns exactly 2; every row has a device that owns 3.
All inputs are finite; a program needn't handle non-finite values. No bound on the sum of `bond_mask` on one device may be relied on, other than what follows from the above.
Results may differ from the reference program's by a relative error of at most 0.0025.
Values may be sent and summed in bfloat16 or wider, within the bound.
A program may use at most 64 MiB of HBM per device.

```python
import jax
import jax.numpy as jnp
from jax import lax

BS = 128
COLS_MEAN = 2
REACH = 4
CMAX = 3
NBC = 64
SLOTS = 96
N_GRP = 8
N_SUB = 4


def draw_ham_columns(key, part):
    base_key = jax.random.fold_in(key, 11)
    couple_key, energy_key = jax.random.split(base_key, 2)
    shape_all = (SLOTS, REACH + 1, BS, BS)
    couplings = jax.random.truncated_normal(couple_key, -4.0, 4.0, shape_all, jnp.float32) * 0.03
    energies = jax.random.uniform(energy_key, (SLOTS, BS), jnp.float32, -2.0, 2.0)
    diagonal = couplings[:, 0]
    symmetric = (diagonal + jnp.swapaxes(diagonal, 1, 2)) * 0.70710677
    eye_mask = jnp.eye(BS, dtype=jnp.float32)
    center_block = symmetric + eye_mask[None, :, :] * energies[:, :, None]
    columns = jnp.concatenate([center_block[:, None], couplings[:, 1:]], axis=1)
    return columns.astype(jnp.bfloat16)


def draw_owned_counts(key, part):
    base_key = jax.random.fold_in(key, 23)
    sign_key, extra_key, forced_key = jax.random.split(base_key, 3)
    pair_count = N_SUB // 2
    sign_values = jax.random.randint(sign_key, (N_GRP, pair_count), 0, 2).astype(jnp.int32) * 2 - 1
    extra = jax.random.randint(extra_key, (N_GRP, pair_count), 0, COLS_MEAN - 1).astype(jnp.int32) + 1
    forced = jax.random.randint(forced_key, (N_GRP,), 0, pair_count).astype(jnp.int32)
    is_forced = jnp.arange(pair_count, dtype=jnp.int32)[None, :] == forced[:, None]
    extra = jnp.where(is_forced, COLS_MEAN - 1, extra)
    sign_values = jnp.where(is_forced, 1, sign_values)
    first_count = COLS_MEAN + sign_values * extra
    second_count = 2 * COLS_MEAN - first_count
    paired = jnp.stack([first_count, second_count], axis=2)
    return paired.reshape(N_GRP, N_SUB).astype(jnp.int32)


def touch_ends(drawn, own_key, least, top_value):
    extent = drawn.shape
    place = [jax.random.randint(jax.random.fold_in(own_key, axis), (), 0, extent[axis]) for axis in range(len(extent))]
    drawn = drawn.at[tuple(place)].set(least)
    longest = extent.index(max(extent))
    place[longest] = (place[longest] + 1) % extent[longest]
    return drawn.at[tuple(place)].set(top_value)


def setup_inputs(seed: int = 0) -> dict:
    splits = jax.random.split(jax.random.key(seed), 5)
    ham_columns = draw_ham_columns(jax.random.fold_in(splits[4], 71), 0)
    bond_mask = touch_ends((jax.random.randint(splits[1], (SLOTS, REACH), 0, 2) < 1).astype(jnp.int32), jax.random.fold_in(splits[1], 1), 0, 1)
    owned_counts = draw_owned_counts(jax.random.fold_in(splits[4], 71), 0)
    fermi_level = jnp.clip(jax.random.uniform(splits[3], (1,), jnp.float32, -0.5, 0.5), -0.5, 0.5)
    return {"ham_columns": ham_columns, "bond_mask": bond_mask, "owned_counts": owned_counts, "fermi_level": fermi_level}


spectral_span = 4.0


def build_tile(window_cols, window_bonds, chemical):
    reach_len = window_bonds.shape[1]
    window_len = window_cols.shape[0]
    block_width = window_cols.shape[2]
    center = reach_len
    identity = jnp.eye(block_width, dtype=jnp.float32)
    bond_values = window_bonds.astype(jnp.float32)
    living = []
    for member in range(window_len):
        if member == center:
            living.append(jnp.ones((), jnp.float32))
        elif member > center:
            living.append(bond_values[center, member - center - 1])
        else:
            living.append(bond_values[member, center - member - 1])
    rows_list = []
    for row_blk in range(window_len):
        pieces = []
        for col_blk in range(window_len):
            distance = row_blk - col_blk
            weight = living[row_blk] * living[col_blk]
            if distance == 0:
                block_value = (window_cols[row_blk, 0].astype(jnp.float32) - chemical * identity) * weight
            elif 0 < distance <= reach_len:
                block_value = window_cols[col_blk, distance].astype(jnp.float32) * (weight * bond_values[col_blk, distance - 1])
            elif 0 < -distance <= reach_len:
                block_value = window_cols[row_blk, -distance].astype(jnp.float32).T * (weight * bond_values[row_blk, -distance - 1])
            else:
                block_value = jnp.zeros((block_width, block_width), jnp.float32)
            pieces.append(block_value)
        rows_list.append(jnp.concatenate(pieces, axis=1))
    return (jnp.concatenate(rows_list, axis=0) / spectral_span).astype(jnp.bfloat16)


def product(matrix, vector):
    return jnp.dot(matrix, vector.astype(jnp.bfloat16), preferred_element_type=jnp.float32)


def apply_first(matrix, vector):
    first_term = product(matrix, vector)
    second = product(matrix, first_term)
    third_term = product(matrix, second)
    return 1.5 * first_term - 0.5 * third_term


def make_selector(window_len, block_width):
    center = (window_len - 1) // 2
    above = jnp.zeros((center * block_width, block_width), jnp.float32)
    return jnp.concatenate([above, jnp.eye(block_width, dtype=jnp.float32), above], axis=0)


def density_column(matrix, selector):
    step_one = apply_first(matrix, selector)
    step_two = apply_first(matrix, step_one)
    step_three = apply_first(matrix, step_two)
    sign_column = 1.5 * step_one - 0.5 * step_three
    return (0.5 * (selector - sign_column)).astype(jnp.bfloat16)


def reference(ham_columns, bond_mask, owned_counts, fermi_level):
    block_width = ham_columns.shape[2]
    reach_len = bond_mask.shape[1]
    window_len = 2 * reach_len + 1
    slot_total = ham_columns.shape[0]
    counts_flat = owned_counts.reshape(-1).astype(jnp.int32)
    run_ends = jnp.cumsum(counts_flat).astype(jnp.int32)
    starts = run_ends - counts_flat
    positions = jnp.arange(NBC, dtype=jnp.int32)
    owner_index = jnp.sum((run_ends[None, :] <= positions[:, None]).astype(jnp.int32), axis=1).astype(jnp.int32)
    slot_of = (owner_index * CMAX + positions - starts[owner_index]).astype(jnp.int32)
    cycle_cols = jnp.take(ham_columns, slot_of, axis=0)
    cycle_bonds = jnp.take(bond_mask, slot_of, axis=0)
    selector = make_selector(window_len, block_width)
    chemical = fermi_level[0]

    def one_center(center_pos):
        window_pos = ((center_pos - reach_len + jnp.arange(window_len, dtype=jnp.int32)) % NBC).astype(jnp.int32)
        matrix = build_tile(jnp.take(cycle_cols, window_pos, axis=0), jnp.take(cycle_bonds, window_pos, axis=0), chemical)
        return density_column(matrix, selector).reshape(window_len, block_width, block_width)

    results = lax.map(one_center, positions)
    slot_ids = jnp.arange(slot_total, dtype=jnp.int32)
    device_of = (slot_ids // CMAX).astype(jnp.int32)
    within = (slot_ids % CMAX).astype(jnp.int32)
    in_use = within < counts_flat[device_of]
    center_of = jnp.minimum(starts[device_of] + within, NBC - 1).astype(jnp.int32)
    picked = jnp.take(results, center_of, axis=0)
    return jnp.where(in_use[:, None, None, None], picked, jnp.zeros_like(picked))
```

```python
import functools

import jax
import jax.numpy as jnp
from jax import lax
from jax.experimental import pallas as pl
from jax.experimental.pallas import tpu as pltpu
from jax.sharding import PartitionSpec as P

MESH = pl.DeviceIdType.MESH
SPAN = 4.0
PAD = 16


def kernel(sizes, ham, bonds, counts, fermi, results, swapped_result,
           win, raw, raw_bonds, band, mask, first, kept, vec_a, vec_b,
           swap_send, swap_recv, out_send, out_recv, send_sem, recv_sem):
    n_grp, n_sub, reach, bs = sizes
    n_win = 2 * reach + 2
    total = n_grp * n_sub
    grp, sub = lax.axis_index("grp"), lax.axis_index("sub")
    me = grp * n_sub + sub
    odd = lax.rem(sub, 2)
    rows = (reach + 1) * bs

    def place(d):
        d = lax.rem(d + total, total)
        return (lax.div(d, n_sub), lax.rem(d, n_sub))

    partner = (grp, sub + 1 - 2 * odd)

    barrier = pltpu.get_barrier_semaphore()
    for shift in (-2, -1, 1, 2):
        pl.semaphore_signal(barrier, inc=1, device_id=place(me + shift), device_id_type=MESH)
    pl.semaphore_wait(barrier, 4)

    slot = 2 - 2 * odd
    swaps = []
    for i, (src, dst) in enumerate(((ham.at[slot], raw), (bonds.at[slot], raw_bonds))):
        swap = pltpu.make_async_remote_copy(
            src_ref=src, dst_ref=dst, send_sem=swap_send.at[i], recv_sem=swap_recv.at[i],
            device_id=partner, device_id_type=MESH)
        swap.start()
        swaps.append(swap)

    mine = counts[grp, sub]
    long_one = (mine > 2).astype(jnp.float32)
    odd_f = odd.astype(jnp.float32)
    c0_slot0 = 1.0 - odd_f
    c0_slot1 = odd_f * long_one
    c0_swap = odd_f * (1.0 - long_one)
    c1_slot1 = (1.0 - odd_f) * long_one
    c1_swap = (1.0 - odd_f) * (1.0 - long_one)
    c1_slot2 = odd_f * long_one
    c1_slot0 = odd_f * (1.0 - long_one)
    chemical = fermi[0]

    eye = (lax.broadcasted_iota(jnp.int32, (bs, bs), 0)
           == lax.broadcasted_iota(jnp.int32, (bs, bs), 1)).astype(jnp.float32)
    for swap in swaps:
        swap.wait()

    zero = jnp.zeros((2 * bs, 2 * bs), jnp.bfloat16)

    def fill(col, sources):
        w = reach + col
        bond = sum(b[...].astype(jnp.float32) * k for b, _, k in sources)
        win[w, rows:rows + PAD, :] = bond.astype(jnp.bfloat16)
        for o in range(reach + 1):
            block = sum(h[o].astype(jnp.float32) * (k * (1.0 / SPAN)) for _, h, k in sources)
            if o == 0:
                block = block - (chemical * (1.0 / SPAN)) * eye
            else:
                block = block * bond[o - 1:o, :]
            win[w, o * bs:(o + 1) * bs, :] = block.astype(jnp.bfloat16)

    fill(0, ((bonds.at[0], ham.at[0], c0_slot0), (bonds.at[1], ham.at[1], c0_slot1),
             (raw_bonds, raw, c0_swap)))
    fill(1, ((bonds.at[0], ham.at[0], c1_slot0), (bonds.at[1], ham.at[1], c1_slot1),
             (bonds.at[2], ham.at[2], c1_slot2), (raw_bonds, raw, c1_swap)))

    plan = []
    c = reach
    plan.append((1, win.at[pl.ds(c, 2)], win.at[pl.ds(c - 2, 2)]))
    plan.append((2, win.at[pl.ds(c, 2)], win.at[pl.ds(c - 4, 2)]))
    for shift in (-1, -2):
        for col in range(2):
            w = c + col - 2 * shift
            part = pl.ds(0, min(reach + 1, n_win - w) * bs)
            plan.append((shift, win.at[c + col, part], win.at[w, part]))
    copies = []
    for i, (shift, src, dst) in enumerate(plan):
        copy = pltpu.make_async_remote_copy(
            src_ref=src, dst_ref=dst, send_sem=send_sem.at[i], recv_sem=recv_sem.at[i],
            device_id=place(me + shift), device_id_type=MESH)
        copy.start()
        copies.append(copy)

    def build(w):
        for o in range(min(reach + 1, n_win - w)):
            block = win[w, o * bs:(o + 1) * bs, :]
            band[(w + o) * bs:(w + o + 1) * bs, w * bs:(w + 1) * bs] = block
            if o:
                band[w * bs:(w + 1) * bs, (w + o) * bs:(w + o + 1) * bs] = block.T

    for w in range(0, n_win - reach - 1, 2):
        v = w + reach + 1
        band[w * bs:(w + 1) * bs, v * bs:(v + 1) * bs] = zero[:bs, :bs]
        band[v * bs:(v + 1) * bs, w * bs:(w + 1) * bs] = zero[:bs, :bs]
    build(c)
    build(c + 1)
    for i, columns in ((0, (c - 2, c - 1)), (2, (c + 2,)), (3, (c + 3,)),
                       (4, (c + 4,)), (5, (c + 5,)), (1, (c - 4, c - 3))):
        copies[i].wait_recv()
        for w in columns:
            build(w)

    one = jnp.ones((1, bs), jnp.float32)
    nil = jnp.zeros((1, bs), jnp.float32)

    def live(center, w):
        distance = abs(w - center)
        if distance == 0:
            return one
        if distance > reach:
            return nil
        tile = win[min(w, center), rows:rows + PAD, :].astype(jnp.float32)
        return tile[distance - 1:distance, :]

    for w in range(n_win):
        mask[w:w + 1, 0:bs] = live(c, w)
        mask[w:w + 1, bs:2 * bs] = live(c + 1, w)

    pairs = n_win // 2

    def masked(r, value):
        top = value[:bs] * mask[2 * r:2 * r + 1, :]
        low = value[bs:] * mask[2 * r + 1:2 * r + 2, :]
        return jnp.concatenate([top, low], axis=0)

    def product(source, r):
        lo = max(0, 2 * r - reach) * bs
        hi = min(n_win, 2 * r + reach + 2) * bs
        value = jnp.dot(band[2 * r * bs:(2 * r + 2) * bs, lo:hi], source[lo:hi, :],
                        preferred_element_type=jnp.float32)
        return masked(r, value)

    def at(r):
        return slice(2 * r * bs, (2 * r + 2) * bs)

    for r in range(pairs):
        value = masked(r, band[at(r), c * bs:(c + 2) * bs].astype(jnp.float32))
        first[at(r), :] = value
        vec_a[at(r), :] = value.astype(jnp.bfloat16)

    for r in range(pairs):
        vec_b[at(r), :] = product(vec_a, r).astype(jnp.bfloat16)
    for r in range(pairs):
        step = 1.5 * first[at(r), :] - 0.5 * product(vec_b, r)
        kept[at(r), :] = step
        vec_a[at(r), :] = step.astype(jnp.bfloat16)

    for r in range(pairs):
        value = product(vec_a, r)
        first[at(r), :] = value
        vec_b[at(r), :] = value.astype(jnp.bfloat16)
    for r in range(pairs):
        vec_a[at(r), :] = product(vec_b, r).astype(jnp.bfloat16)
    for r in range(pairs):
        step = 1.5 * first[at(r), :] - 0.5 * product(vec_a, r)
        vec_b[at(r), :] = step.astype(jnp.bfloat16)

    for r in range(pairs):
        value = product(vec_b, r)
        first[at(r), :] = value
        vec_a[at(r), :] = value.astype(jnp.bfloat16)
    for r in range(pairs):
        vec_b[at(r), :] = product(vec_a, r).astype(jnp.bfloat16)
    for r in range(pairs):
        step = 1.5 * first[at(r), :] - 0.5 * product(vec_b, r)
        sign = 1.5 * kept[at(r), :] - 0.5 * step
        for half in range(2):
            w = 2 * r + half
            for k in range(2):
                if not 0 <= w - k <= 2 * reach:
                    continue
                value = -0.5 * sign[half * bs:(half + 1) * bs, k * bs:(k + 1) * bs]
                if w == c + k:
                    value = 0.5 * eye + value
                results[k, w - k] = value.astype(jnp.bfloat16)

    swap = pltpu.make_async_remote_copy(
        src_ref=results.at[1 - odd], dst_ref=swapped_result,
        send_sem=out_send, recv_sem=out_recv, device_id=partner, device_id_type=MESH)
    swap.start()
    for copy in copies:
        copy.wait_send()
    swap.wait()


def body(n_grp, n_sub, ham_columns, bond_mask, owned_counts, fermi_level):
    slots, depth, bs, _ = ham_columns.shape
    reach = depth - 1
    n_win = 2 * reach + 2
    vmem, smem = pltpu.VMEM, pltpu.SMEM
    wide = jnp.pad(bond_mask.astype(jnp.bfloat16), ((0, 0), (0, PAD - reach)))
    wide = jnp.broadcast_to(wide[:, :, None], (slots, PAD, bs))
    sizes = (n_grp, n_sub, reach, bs)
    results, swapped = pl.pallas_call(
        functools.partial(kernel, sizes),
        out_shape=(
            jax.ShapeDtypeStruct((2, 2 * reach + 1, bs, bs), jnp.bfloat16),
            jax.ShapeDtypeStruct((2 * reach + 1, bs, bs), jnp.bfloat16),
        ),
        in_specs=[
            pl.BlockSpec(memory_space=vmem), pl.BlockSpec(memory_space=vmem),
            pl.BlockSpec(memory_space=smem), pl.BlockSpec(memory_space=smem),
        ],
        out_specs=(pl.BlockSpec(memory_space=vmem), pl.BlockSpec(memory_space=vmem)),
        scratch_shapes=[
            vmem((n_win, depth * bs + PAD, bs), jnp.bfloat16),
            vmem((depth, bs, bs), jnp.bfloat16),
            vmem((PAD, bs), jnp.bfloat16),
            vmem((n_win * bs, n_win * bs), jnp.bfloat16),
            vmem((16, 2 * bs), jnp.float32),
            vmem((n_win * bs, 2 * bs), jnp.float32),
            vmem((n_win * bs, 2 * bs), jnp.float32),
            vmem((n_win * bs, 2 * bs), jnp.bfloat16),
            vmem((n_win * bs, 2 * bs), jnp.bfloat16),
            pltpu.SemaphoreType.DMA((2,)),
            pltpu.SemaphoreType.DMA((2,)),
            pltpu.SemaphoreType.DMA,
            pltpu.SemaphoreType.DMA,
            pltpu.SemaphoreType.DMA((6,)),
            pltpu.SemaphoreType.DMA((6,)),
        ],
        compiler_params=pltpu.CompilerParams(collective_id=0, has_side_effects=True),
    )(ham_columns, wide, owned_counts, fermi_level)

    grp, sub = lax.axis_index("grp"), lax.axis_index("sub")
    odd = (sub % 2) == 1
    long_one = owned_counts[grp, sub] > 2
    none = jnp.zeros_like(swapped)
    slot0 = jnp.where(odd, jnp.where(long_one, swapped, results[1]), results[0])
    slot1 = jnp.where(long_one, jnp.where(odd, results[0], results[1]), none)
    slot2 = jnp.where(long_one, jnp.where(odd, results[1], swapped), none)
    return jnp.stack([slot0, slot1, slot2])


def solution(mesh):
    n_grp, n_sub = mesh.shape["grp"], mesh.shape["sub"]
    placed = (P(("grp", "sub"), None, None, None), P(("grp", "sub"), None), P(), P())
    return jax.shard_map(
        functools.partial(body, n_grp, n_sub),
        mesh=mesh,
        in_specs=placed,
        out_specs=P(("grp", "sub"), None, None, None),
        check_vma=False,
    )
```

```python
import functools

import jax
import jax.numpy as jnp
from jax import lax
from jax.experimental import pallas as pl
from jax.experimental.pallas import tpu as pltpu
from jax.sharding import PartitionSpec as P

MESH = pl.DeviceIdType.MESH
SPAN = 4.0
PAD = 16


def kernel(sizes, ham_hbm, bonds_hbm, counts_hbm, fermi_hbm, out,
           ham, bonds, counts, fermi, win, raw, raw_bonds, band, mask, first, kept,
           vec_a, vec_b, results, swapped_result,
           load_sem, swap_send, swap_recv, out_send, out_recv, send_sem, recv_sem):
    n_grp, n_sub, reach, bs = sizes
    n_win = 2 * reach + 2
    total = n_grp * n_sub
    grp, sub = lax.axis_index("grp"), lax.axis_index("sub")
    me = grp * n_sub + sub
    odd = lax.rem(sub, 2)
    even = 1 - odd
    rows = (reach + 1) * bs
    c = reach

    def place(shift):
        d = lax.rem(me + shift + total, total)
        return (lax.div(d, n_sub), lax.rem(d, n_sub))

    barrier = pltpu.get_barrier_semaphore()
    for shift in (-2, -1, 1, 2):
        pl.semaphore_signal(barrier, inc=1, device_id=place(shift), device_id_type=MESH)

    loads = []
    for i, (src, dst) in enumerate(((counts_hbm, counts), (fermi_hbm, fermi),
                                    (bonds_hbm, bonds), (ham_hbm, ham))):
        load = pltpu.make_async_copy(src, dst, load_sem.at[i])
        load.start()
        loads.append(load)
    zero = jnp.zeros((bs, bs), jnp.bfloat16)
    for w in range(0, n_win - reach - 1, 2):
        v = w + reach + 1
        band[w * bs:(w + 1) * bs, v * bs:(v + 1) * bs] = zero
        band[v * bs:(v + 1) * bs, w * bs:(w + 1) * bs] = zero
    eye = (lax.broadcasted_iota(jnp.int32, (bs, bs), 0)
           == lax.broadcasted_iota(jnp.int32, (bs, bs), 1)).astype(jnp.float32)
    for load in loads:
        load.wait()

    long_one = (counts[grp, sub] > 2).astype(jnp.float32)
    odd_f = odd.astype(jnp.float32)
    chemical = fermi[0]

    def fill(w, sources):
        bond = []
        for o in range(reach):
            lane = sum(b.astype(jnp.float32) * k for b, _, k in sources)
            bond.append(jnp.broadcast_to(lane[:, o:o + 1], (1, bs)))
        tile = jnp.concatenate(bond + [jnp.zeros((PAD - reach, bs), jnp.float32)], axis=0)
        win[w, rows:rows + PAD, :] = tile.astype(jnp.bfloat16)
        for o in range(reach + 1):
            block = sum(h[o].astype(jnp.float32) * (k * (1.0 / SPAN)) for _, h, k in sources)
            if o == 0:
                block = block - (chemical * (1.0 / SPAN)) * eye
            else:
                block = block * bond[o - 1]
            win[w, o * bs:(o + 1) * bs, :] = block.astype(jnp.bfloat16)

    last = odd_f * long_one
    fill(c + odd, ((bonds[0:1, :], ham.at[0], 1.0 - last), (bonds[2:3, :], ham.at[2], last)))

    pl.semaphore_wait(barrier, 4)

    def remote(src, dst, send, recv, device):
        return pltpu.make_async_remote_copy(
            src_ref=src, dst_ref=dst, send_sem=send, recv_sem=recv,
            device_id=device, device_id_type=MESH)

    partner = (grp, sub + 1 - 2 * odd)
    swaps = [remote(ham_hbm.at[2 * even], raw, swap_send.at[0], swap_recv.at[0], partner),
             remote(bonds_hbm, raw_bonds, swap_send.at[1], swap_recv.at[1], partner)]
    for swap in swaps:
        swap.start()

    def part(w):
        if w < c:
            return pl.ds(0, rows + PAD)
        return pl.ds(0, min(reach + 1, n_win - w) * bs)

    def column(i, source, w, shift):
        return remote(win.at[source, part(w)], win.at[w, part(w)],
                      send_sem.at[i], recv_sem.at[w], place(shift))

    def arrive(w):
        column(0, w, w, 1).wait_recv()

    sends_even = ((c, c - 4, 2), (c, c + 2, -1), (c, c - 2, 1))
    sends_odd = ((c + 1, c - 3, 2), (c + 1, c + 5, -2), (c + 1, c + 3, -1))
    later_even = ((c + 1, c - 3, 2), (c + 1, c + 3, -1), (c + 1, c - 1, 1))
    later_odd = ((c, c - 2, 1), (c, c + 4, -2), (c, c + 2, -1))

    @pl.when(odd == 0)
    def _():
        for i, send in enumerate(sends_even):
            column(i, *send).start()

    @pl.when(odd == 1)
    def _():
        for i, send in enumerate(sends_odd):
            column(i, *send).start()

    for swap in swaps:
        swap.wait()
    fill(c + even, ((bonds[1:2, :], ham.at[1], long_one),
                    (jnp.where(odd == 0, raw_bonds[0:1, :], raw_bonds[2:3, :]), raw, 1.0 - long_one)))

    @pl.when(odd == 0)
    def _():
        for i, send in enumerate(later_even):
            column(3 + i, *send).start()

    @pl.when(odd == 1)
    def _():
        for i, send in enumerate(later_odd):
            column(3 + i, *send).start()

    def build(w):
        for o in range(min(reach + 1, n_win - w)):
            block = win[w, o * bs:(o + 1) * bs, :]
            band[(w + o) * bs:(w + o + 1) * bs, w * bs:(w + 1) * bs] = block
            if o:
                band[w * bs:(w + 1) * bs, (w + o) * bs:(w + o + 1) * bs] = block.T

    build(c)
    build(c + 1)

    relay_even = {c - 2: (6, c - 2, c - 4, 1)}
    relay_odd = {c - 3: (6, c - 3, c - 1, -1), c + 2: (7, c + 2, c + 4, -1), c + 3: (8, c + 3, c + 5, -1)}

    @pl.when(odd == 0)
    def _():
        for w in (c + 2, c + 3, c - 4, c - 2, c - 3, c - 1, c + 4, c + 5):
            arrive(w)
            if w in relay_even:
                column(*relay_even[w]).start()
            build(w)

    @pl.when(odd == 1)
    def _():
        for w in (c - 2, c - 1, c - 3, c + 2, c + 3, c + 5, c + 4, c - 4):
            arrive(w)
            if w in relay_odd:
                column(*relay_odd[w]).start()
            build(w)

    one = jnp.ones((1, bs), jnp.float32)
    nil = jnp.zeros((1, bs), jnp.float32)

    def live(center, w):
        distance = abs(w - center)
        if distance == 0:
            return one
        if distance > reach:
            return nil
        tile = win[min(w, center), rows:rows + PAD, :].astype(jnp.float32)
        return tile[distance - 1:distance, :]

    for w in range(n_win):
        mask[w:w + 1, 0:bs] = live(c, w)
        mask[w:w + 1, bs:2 * bs] = live(c + 1, w)

    pairs = n_win // 2

    def give(i):
        span = pl.ds(0, reach + 1) if i == 0 else pl.ds(reach + 1, reach)
        return remote(results.at[even, span], swapped_result.at[span],
                      out_send.at[i], out_recv.at[i], partner)

    def masked(r, value):
        top = value[:bs] * mask[2 * r:2 * r + 1, :]
        low = value[bs:] * mask[2 * r + 1:2 * r + 2, :]
        return jnp.concatenate([top, low], axis=0)

    def product(source, r):
        lo = max(0, 2 * r - reach) * bs
        hi = min(n_win, 2 * r + reach + 2) * bs
        value = jnp.dot(band[2 * r * bs:(2 * r + 2) * bs, lo:hi], source[lo:hi, :],
                        preferred_element_type=jnp.float32)
        return masked(r, value)

    def at(r):
        return slice(2 * r * bs, (2 * r + 2) * bs)

    for r in range(pairs):
        value = masked(r, band[at(r), c * bs:(c + 2) * bs].astype(jnp.float32))
        first[at(r), :] = value
        vec_a[at(r), :] = value.astype(jnp.bfloat16)

    for r in range(pairs):
        vec_b[at(r), :] = product(vec_a, r).astype(jnp.bfloat16)
    for r in range(pairs):
        step = 1.5 * first[at(r), :] - 0.5 * product(vec_b, r)
        kept[at(r), :] = step
        vec_a[at(r), :] = step.astype(jnp.bfloat16)

    for r in range(pairs):
        value = product(vec_a, r)
        first[at(r), :] = value
        vec_b[at(r), :] = value.astype(jnp.bfloat16)
    for r in range(pairs):
        vec_a[at(r), :] = product(vec_b, r).astype(jnp.bfloat16)
    for r in range(pairs):
        step = 1.5 * first[at(r), :] - 0.5 * product(vec_a, r)
        vec_b[at(r), :] = step.astype(jnp.bfloat16)

    for r in range(pairs):
        value = product(vec_b, r)
        first[at(r), :] = value
        vec_a[at(r), :] = value.astype(jnp.bfloat16)
    for r in range(pairs):
        vec_b[at(r), :] = product(vec_a, r).astype(jnp.bfloat16)
    for r in range(pairs):
        step = 1.5 * first[at(r), :] - 0.5 * product(vec_b, r)
        sign = 1.5 * kept[at(r), :] - 0.5 * step
        for half in range(2):
            w = 2 * r + half
            for k in range(2):
                if not 0 <= w - k <= 2 * reach:
                    continue
                value = -0.5 * sign[half * bs:(half + 1) * bs, k * bs:(k + 1) * bs]
                if w == c + k:
                    value = 0.5 * eye + value
                results[k, w - k] = value.astype(jnp.bfloat16)
        if r == reach // 2:
            give(0).start()
    give(1).start()

    even_f, short = 1.0 - odd_f, 1.0 - long_one
    places = ((even_f, odd_f * short, odd_f * long_one),
              (odd_f * long_one, even_f * long_one, None),
              (None, odd_f * long_one, even_f * long_one))

    def write(t, w):
        terms = (results[0, w], results[1, w], swapped_result[w])
        value = sum(k * x.astype(jnp.float32) for k, x in zip(places[t], terms) if k is not None)
        out[t, w] = value.astype(jnp.bfloat16)

    def finish(sends):
        for i, send in enumerate(sends):
            column(i, *send).wait_send()

    @pl.when(odd == 0)
    def _():
        finish(sends_even + later_even + tuple(v[1:] for v in relay_even.values()))

    @pl.when(odd == 1)
    def _():
        finish(sends_odd + later_odd + tuple(v[1:] for v in relay_odd.values()))

    for w in range(2 * reach + 1):
        write(1, w)
    give(0).wait()
    for w in range(reach + 1):
        write(0, w)
        write(2, w)
    give(1).wait()
    for w in range(reach + 1, 2 * reach + 1):
        write(0, w)
        write(2, w)


def body(n_grp, n_sub, ham_columns, bond_mask, owned_counts, fermi_level):
    slots, depth, bs, _ = ham_columns.shape
    reach = depth - 1
    n_win = 2 * reach + 2
    vmem, smem, dma = pltpu.VMEM, pltpu.SMEM, pltpu.SemaphoreType.DMA
    sizes = (n_grp, n_sub, reach, bs)
    return pl.pallas_call(
        functools.partial(kernel, sizes),
        out_shape=jax.ShapeDtypeStruct((slots, 2 * reach + 1, bs, bs), jnp.bfloat16),
        in_specs=[pl.BlockSpec(memory_space=pl.ANY)] * 4,
        out_specs=pl.BlockSpec(memory_space=vmem),
        scratch_shapes=[
            vmem(ham_columns.shape, jnp.bfloat16),
            vmem(bond_mask.shape, jnp.int32),
            smem(owned_counts.shape, jnp.int32),
            smem(fermi_level.shape, jnp.float32),
            vmem((n_win, depth * bs + PAD, bs), jnp.bfloat16),
            vmem((depth, bs, bs), jnp.bfloat16),
            vmem(bond_mask.shape, jnp.int32),
            vmem((n_win * bs, n_win * bs), jnp.bfloat16),
            vmem((16, 2 * bs), jnp.float32),
            vmem((n_win * bs, 2 * bs), jnp.float32),
            vmem((n_win * bs, 2 * bs), jnp.float32),
            vmem((n_win * bs, 2 * bs), jnp.bfloat16),
            vmem((n_win * bs, 2 * bs), jnp.bfloat16),
            vmem((2, 2 * reach + 1, bs, bs), jnp.bfloat16),
            vmem((2 * reach + 1, bs, bs), jnp.bfloat16),
            dma((4,)),
            dma((2,)),
            dma((2,)),
            dma((2,)),
            dma((2,)),
            dma((9,)),
            dma((n_win,)),
        ],
        compiler_params=pltpu.CompilerParams(collective_id=0, has_side_effects=True),
    )(ham_columns, bond_mask, owned_counts, fermi_level)


def solution(mesh):
    n_grp, n_sub = mesh.shape["grp"], mesh.shape["sub"]
    placed = (P(("grp", "sub"), None, None, None), P(("grp", "sub"), None), P(), P())
    return jax.shard_map(
        functools.partial(body, n_grp, n_sub),
        mesh=mesh,
        in_specs=placed,
        out_specs=P(("grp", "sub"), None, None, None),
        check_vma=False,
    )
```
